32 devices in a mesh: groups: 2 (over x), tm: 16 (over z, y, core).
Axes of the slice: x: 2, y: 2, z: 4, core: 2. Of those that a mesh axis runs over, the one named last changes fastest.
Arguments:
- points: float32 [32, 64, 2048], P(('groups', 'tm')), parts along dimension 0, may hold values from -4 to 4
- potentials: float32 [32, 224, 2048], P(('groups', 'tm')), parts along dimension 0, may hold values from 0.5 to 25, as said below
- supports: int32 [32], P(('groups', 'tm')), parts along dimension 0, may hold values from 512 to 2048, as said below
Outputs:
- messages: float32 [32, 224, 2048], P(('groups', 'tm')), parts along dimension 0
- log_scale: float32 [448], P('groups'), parts along dimension 0
The draws below stay inside these ranges and needn't reach their ends.
There are 2 independent parts, one for each index of `groups`. The reference program is written for one: setup_inputs(seed, part) draws one part's arguments, and reference() takes and returns one part's arrays. A program takes and returns all parts, laid end to end along the dimension named above; each array names one. Nothing has to cross between parts.
Inputs may be any that keep to these rules, and one draw needn't show every extreme that they name: `supports`: the first and the last time slice have all 2048 points live; every other slice has between 512 and 1024 live points, at its first positions. `potentials`: positive scalings.
All inputs are finite; a program needn't handle non-finite values.
Results may differ from the reference program's by a relative error of at most 0.017.
Values may be sent and summed in bfloat16 or wider, within the bound.
No kernel may reach another device: no remote copies, remote signals or barrier semaphores. Data moves between devices by JAX's collectives and lax.ppermute only.
A program may use at most 64 MiB of HBM per device.

```python
import jax
import jax.numpy as jnp
from jax import lax

DIM = 64
PTS = 2048
COLS = 224
SLICES = 16


def draw_points(key, part):
    first_key, second_key = jax.random.split(key, 2)
    start = jax.random.normal(first_key, (DIM, PTS), jnp.float32)
    innovations = 0.6 * jax.random.normal(second_key, (SLICES - 1, DIM, PTS), jnp.float32)
    start = jnp.clip(start, -4.0, 4.0)

    def advance(previous, innovation):
        following = jnp.clip(0.8 * previous + innovation, -4.0, 4.0)
        return (following, following)
    unused, later = lax.scan(advance, start, innovations)
    return jnp.concatenate([start[None], later], axis=0)


def draw_potentials(key, part):
    inner_key = jax.random.fold_in(key, 7)
    places = jnp.arange(SLICES).astype(jnp.float32) / (SLICES - 1)
    rough = jnp.exp(jax.random.uniform(inner_key, (SLICES, COLS, PTS), jnp.float32, -0.6931472, 0.6931472))
    growth = 1.5
    ramp = jnp.exp(growth * places)
    return rough * ramp[:, None, None]


def draw_supports(key, part):
    inner = jax.random.randint(key, (SLICES,), PTS // 4, PTS // 2 + 1)
    places = jnp.arange(SLICES)
    ends = (places == 0) | (places == SLICES - 1)
    return jnp.where(ends, PTS, inner).astype(jnp.int32)


def setup_inputs(seed: int = 0, part: int = 0) -> dict:
    arg_keys = jax.random.split(jax.random.key(seed), 4)
    part_keys = jax.random.split(jax.random.fold_in(arg_keys[3], part), 4)
    return {
        "points": draw_points(jax.random.fold_in(jax.random.fold_in(arg_keys[3], part), 71), part),
        "potentials": draw_potentials(jax.random.fold_in(jax.random.fold_in(arg_keys[3], part), 71), part),
        "supports": draw_supports(jax.random.fold_in(jax.random.fold_in(arg_keys[3], part), 71), part),
    }


A_DECAY = 0.8
EPS_SCALE = 0.05


def slice_kernel(source, target):
    dim_count, point_count = source.shape
    block_rows = min(512, point_count)
    inv_width = 1.0 / (2.0 * EPS_SCALE * dim_count)
    target_sq = jnp.sum(target * target, axis=0)
    pieces = jnp.transpose(source.reshape(dim_count, point_count // block_rows, block_rows), (1, 0, 2))

    def one_block(segment):
        products = lax.dot_general(segment, target, (((0,), (0,)), ((), ())), precision=lax.Precision.HIGHEST, preferred_element_type=jnp.float32)
        segment_sq = jnp.sum(segment * segment, axis=0)
        distance = target_sq[None, :] + (A_DECAY * A_DECAY) * segment_sq[:, None] - (2.0 * A_DECAY) * products
        return jnp.exp(-inv_width * distance).astype(jnp.bfloat16)

    return lax.map(one_block, pieces).reshape(point_count, point_count)


def reference(points, potentials, supports):
    slices, dim_count, point_count = points.shape
    live_mask = (jnp.arange(point_count)[None, :] < supports[:, None]).astype(jnp.float32)
    counts = supports.astype(jnp.float32)
    start_msg = jnp.broadcast_to(live_mask[0][None, :], (potentials.shape[1], point_count)).astype(jnp.float32)

    def advance(message, inputs):
        source, target, potential, live_row, support = inputs
        weighted = (message * potential).astype(jnp.bfloat16)
        kernel = slice_kernel(source, target)
        pushed = jnp.dot(weighted.astype(jnp.float32), kernel.astype(jnp.float32), precision=lax.Precision.HIGHEST, preferred_element_type=jnp.float32) * live_row[None, :]
        column_sum = jnp.sum(pushed, axis=1)
        following = pushed * (support / column_sum)[:, None]
        return following, (following, jnp.log(column_sum / support))

    unused, (later, log_terms) = lax.scan(advance, start_msg, (points[:-1], points[1:], potentials[:-1], live_mask[1:], counts[1:]))
    messages = jnp.concatenate([start_msg[None], later], axis=0)
    log_scale = jnp.sum(log_terms, axis=0) / (slices - 1)
    return messages, log_scale
```

```python
import functools
import math

import jax
import jax.numpy as jnp
from jax import lax
from jax.experimental import pallas as pl
from jax.experimental.pallas import tpu as pltpu
from jax.sharding import PartitionSpec as P

A_DECAY = 0.8
EPS_SCALE = 0.05
LIVE = 1024
TEAM = 8
BLOCK = 32
LOGS = 128
SUP = 8
DEAD = -1e30

F32 = jnp.float32
BF16 = jnp.bfloat16
VMEM = pl.BlockSpec(memory_space=pltpu.VMEM)


def params(mib, grid=False):
    semantics = ("arbitrary",) if grid else None
    return pltpu.CompilerParams(vmem_limit_bytes=mib << 20, dimension_semantics=semantics)


def block_of(device):
    return (device & 1) * 4 + (device >> 1)


def split2(value):
    high = value.astype(BF16)
    return high, (value - high.astype(F32)).astype(BF16)


def split3(value):
    high = value.astype(BF16).astype(F32)
    rest = value - high
    middle = rest.astype(BF16).astype(F32)
    return high, middle, rest - middle


def rows_of(parts):
    width = parts[0].shape[1]
    filler = jnp.zeros((16 - len(parts), width), F32)
    return jnp.concatenate([*parts, filler], axis=0).astype(BF16)


def source_features(points):
    unit = math.log2(math.e) / (2.0 * EPS_SCALE * points.shape[0])
    high, low = split2(points * (2.0 * A_DECAY * unit))
    square = jnp.sum(points * points, axis=0, keepdims=True) * (-A_DECAY * A_DECAY * unit)
    one = jnp.ones_like(square)
    return jnp.concatenate([high, high, low, rows_of((*split3(square), one, one, one))], axis=0)


def target_features(points, support, first=0):
    unit = math.log2(math.e) / (2.0 * EPS_SCALE * points.shape[0])
    high, low = split2(points)
    square = jnp.sum(points * points, axis=0, keepdims=True) * (-unit)
    one = jnp.ones_like(square)
    place = lax.broadcasted_iota(jnp.int32, square.shape, 1).astype(F32) + first
    live = place < support
    top, middle, rest = split3(square)
    top = jnp.where(live, top, DEAD)
    middle = jnp.where(live, middle, 0.0)
    rest = jnp.where(live, rest, 0.0)
    return jnp.concatenate([high, low, high, rows_of((one, one, one, top, middle, rest))], axis=0)


def fill_kernel(source, target, support, turned, features, write, first=0):
    turned[...] = source_features(source).T
    features[...] = target_features(target, support, first)
    step = 256
    for start in range(0, source.shape[1], step):
        exponent = jnp.dot(
            turned[start : start + step, :], features[...], preferred_element_type=F32
        )
        write(start, step, jnp.exp2(exponent).astype(BF16))


def log_lanes(logs):
    lane = lax.broadcasted_iota(jnp.int32, (logs.shape[0], LOGS), 1)
    high, middle, rest = split3(logs)
    third = jnp.where(lane == 2, rest, 0.0)
    return jnp.where(lane == 0, high, jnp.where(lane == 1, middle, third)).astype(BF16)


def first_step(own_ref, other_ref, pot_own, pot_other, sup_ref, *refs):
    outs, message_ref, source, target, pot_first, pot_next, turned, features, kernel = (
        refs[:4],
        *refs[4:],
    )
    position = lax.axis_index("tm")

    @pl.when(position == 0)
    def _():
        source[...] = own_ref[...]
        target[...] = other_ref[:, :LIVE]
        pot_first[...] = pot_own[...]
        pot_next[...] = pot_other[:, :LIVE]

    @pl.when(position == 1)
    def _():
        source[...] = other_ref[...]
        target[...] = own_ref[:, :LIVE]
        pot_first[...] = pot_other[...]
        pot_next[...] = pot_own[:, :LIVE]

    @pl.when(position < 2)
    def _():
        support = sup_ref[0]

        def write(start, size, values):
            kernel[start : start + size, :] = values

        fill_kernel(source[...], target[...], support, turned, features, write)
        pushed = jnp.dot(pot_first[...], kernel[...], preferred_element_type=F32)
        total = jnp.sum(pushed, axis=1, keepdims=True)
        message = pushed * (support / total)
        message_ref[...] = message.astype(BF16)
        weighted = (message * pot_next[...].astype(F32)).astype(BF16)
        logs = log_lanes(jnp.log(total / support))
        for index, out in enumerate(outs):
            rows = slice(index * BLOCK, (index + 1) * BLOCK)
            out[:, :LIVE] = weighted[rows]
            out[:, LIVE:] = logs[rows]


def split_pots(pot_ref, *outs):
    device = lax.axis_index("tm") % TEAM
    last = pot_ref.shape[0] // BLOCK - 1
    for mask, out in enumerate(outs):
        row = pl.multiple_of(jnp.minimum(block_of(device ^ mask), last) * BLOCK, BLOCK)
        out[...] = pot_ref[pl.ds(row, BLOCK), :].astype(BF16)


def build(last_position, *refs):
    slots, tail_ref = refs[:TEAM], refs[TEAM]
    kernel_ref, seventh_ref, sup_ref, sums_ref = refs[TEAM + 1 : TEAM + 5]
    points, turned, features = refs[TEAM + 5 :]
    position = lax.axis_index("tm")
    device, team = position % TEAM, position // TEAM
    last_team = last_position // TEAM
    dims = tail_ref.shape[0]
    step = pl.program_id(0)

    @pl.when(step == 0)
    def _():
        for mask, slot in enumerate(slots):
            points[device ^ mask] = slot[...]
        for index in range(TEAM):
            sup_ref[index : index + 1, :] = points[index, dims : dims + 1, :LOGS]
        seventh_ref[...] = points[TEAM - 1]
        sums_ref[...] = jnp.zeros_like(sums_ref)

    def write(start, size, values):
        kernel_ref[0, start : start + size, :] = values

    inner = (step < TEAM - 1) & ((team > 0) | (step > 1)) & (step > 0)
    closing = (step == TEAM - 1) & ((team < last_team) | (position == last_position))

    @pl.when(inner | closing)
    def _():
        fill_kernel(
            points[step - 1, :dims, :],
            points[step, :dims, :],
            points[step, dims, 0],
            turned,
            features,
            write,
        )

    @pl.when((step == TEAM) & (position == last_position))
    def _():
        fill_kernel(
            points[TEAM - 2, :dims, :],
            tail_ref[...],
            points[TEAM - 1, dims, 0],
            turned,
            features,
            write,
            first=LIVE,
        )

    @pl.when((step >= TEAM - 1) & (position == last_position))
    def _():
        one = jnp.ones((8, LIVE), BF16)
        sums_ref[...] += lax.dot_general(
            one, kernel_ref[0], (((1,), (1,)), ((), ())), preferred_element_type=F32
        )


def bridge(before_ref, start_ref, kernel_ref, turned, features):
    @pl.when(lax.axis_index("tm") >= TEAM)
    def _():
        def write(start, size, values):
            kernel_ref[start : start + size, :] = values

        dims = before_ref.shape[0] - SUP
        fill_kernel(
            before_ref[:dims, :],
            start_ref[:dims, :],
            start_ref[dims, 0],
            turned,
            features,
            write,
        )


def sweep(stage, last_team, carried, arrivals, flag_ref, *refs):
    refs = list(refs)

    def take(count):
        taken = refs[:count]
        del refs[:count]
        return taken

    kernel_ref, opening_ref, sup_ref, sums_ref = take(4)
    pots = take(TEAM)
    incoming = take(arrivals)
    previous = take(TEAM if carried else 0)
    outs = take(TEAM)
    (leave_ref,) = take(1)
    weighted, logs, pot_all, stored = refs
    position = lax.axis_index("tm")
    device, team = position % TEAM, position // TEAM
    step = pl.program_id(0)
    first = 0 if stage else 2
    final = TEAM - 2 if stage == last_team else TEAM - 1
    active = team == stage

    @pl.when(active & (step == first))
    def _():
        for mask, pot in enumerate(pots):
            pot_all[device ^ mask] = pot[...]

        def load(ref):
            weighted[...] = ref[:, :LIVE]
            total = jnp.sum(ref[:, LIVE:].astype(F32), axis=1, keepdims=True)
            logs[...] = jnp.broadcast_to(total, logs.shape)

        if arrivals == 1:
            load(incoming[0])
        else:
            for index, ref in enumerate(incoming):
                pl.when(device >> 1 == index)(functools.partial(load, ref))

    def advance(kernel):
        support = sup_ref[pl.ds(step, 1), 0:1]
        pushed = jnp.dot(weighted[...], kernel, preferred_element_type=F32)
        total = jnp.sum(pushed, axis=1, keepdims=True)
        message = pushed * (support / total)
        stored[step] = message.astype(BF16)
        weighted[...] = (message * pot_all[step].astype(F32)).astype(BF16)
        logs[...] += jnp.log(total / support)

    if stage:
        pl.when(active & (step == 0))(lambda: advance(opening_ref[...]))
    inner = (step >= max(first, 1)) & (step <= final)
    pl.when(active & inner)(lambda: advance(kernel_ref[0]))

    @pl.when(active & (step == TEAM - 1))
    def _():
        if stage == last_team:
            support = sup_ref[TEAM - 1 : TEAM, 0:1]
            reach = jnp.sum(
                weighted[...].astype(F32) * sums_ref[0:1, :], axis=1, keepdims=True
            )
            logs[...] += jnp.log(reach / support)
            stored[TEAM - 1] = weighted[...]
        lanes = log_lanes(logs[:, 0:1])
        for mask, out in enumerate(outs):
            out[:, :LIVE] = stored[device ^ mask]
            out[:, LIVE:] = lanes
        leave_ref[:, :LIVE] = weighted[...]
        leave_ref[:, LIVE:] = lanes

    if carried:

        @pl.when((team != stage) & (step == TEAM - 1))
        def _():
            for source, out in zip(previous, outs):
                out[...] = source[...]


def gather_logs(scale, *refs):
    blocks, out_ref, column = refs[:TEAM], refs[TEAM], refs[TEAM + 1]
    device = lax.axis_index("tm") % TEAM
    for mask, block in enumerate(blocks):
        total = jnp.sum(block[...].astype(F32), axis=1, keepdims=True) * scale
        row = pl.multiple_of(block_of(device ^ mask) * BLOCK, BLOCK)
        column[pl.ds(row, BLOCK), :] = jnp.broadcast_to(total, (BLOCK, LOGS))
    out_ref[...] = column[...].T[0:8, :]


def finish(last_position, *refs):
    blocks = refs[:TEAM]
    early_own, early_other, sup_ref, kernel_ref, out_ref, weighted, halves, sem = refs[TEAM:]
    position = lax.axis_index("tm")
    device = position % TEAM
    spare = out_ref.shape[1] - LIVE
    columns = out_ref.shape[0]

    @pl.when(position == 0)
    def _():
        place = lax.broadcasted_iota(jnp.int32, out_ref.shape, 1)
        out_ref[...] = jnp.where(place < sup_ref[0], 1.0, 0.0)

    @pl.when(position == 1)
    def _():
        cut = 4 * BLOCK
        out_ref[:cut, :LIVE] = early_other[...].astype(F32)
        out_ref[cut:, :LIVE] = early_own[: columns - cut, :].astype(F32)
        out_ref[:, LIVE:] = jnp.zeros((columns, spare), F32)

    @pl.when((position > 1) & (position < last_position))
    def _():
        for mask, block in enumerate(blocks):

            @pl.when(device ^ mask < TEAM - 1)
            def _():
                row = pl.multiple_of(block_of(device ^ mask) * BLOCK, BLOCK)
                out_ref[pl.ds(row, BLOCK), :LIVE] = block[:, :LIVE].astype(F32)

        out_ref[:, LIVE:] = jnp.zeros((columns, spare), F32)

    @pl.when(position == last_position)
    def _():
        copies = []
        for half in range(2):
            copy = pltpu.make_async_copy(
                kernel_ref.at[TEAM - 1 + half], halves.at[half], sem.at[half]
            )
            copy.start()
            copies.append(copy)
        for mask in range(1, TEAM):
            row = block_of(TEAM - 1 - mask) * BLOCK
            weighted[row : row + BLOCK, :] = blocks[mask][:, :LIVE]
        total = jnp.zeros((columns, 1), F32)
        for half, copy in enumerate(copies):
            copy.wait()
            pushed = jnp.dot(weighted[...], halves[half], preferred_element_type=F32)
            out_ref[:, half * LIVE : (half + 1) * LIVE] = pushed
            total = total + jnp.sum(pushed, axis=1, keepdims=True)
        ratio = sup_ref[0].astype(F32) / total
        out_ref[...] = out_ref[...] * ratio


def shape(*dims, dtype=BF16):
    return jax.ShapeDtypeStruct(dims, dtype)


def scratch(*dims, dtype=BF16):
    return pltpu.VMEM(dims, dtype)


def per_device(points, potentials, supports):
    points, potentials = points[0], potentials[0]
    dims, count = points.shape
    columns = potentials.shape[0]
    devices = lax.axis_size("tm")
    position = lax.axis_index("tm")
    last = devices - 1
    teams = devices // TEAM
    depth = 3 * dims + 16
    smem = pl.BlockSpec(memory_space=pltpu.SMEM)
    anywhere = pl.BlockSpec(memory_space=pl.ANY)

    def move(value, pairs):
        return lax.ppermute(value, "tm", pairs)

    def swap(value, mask, keep=lambda source, target: True):
        pairs = [(i, i ^ mask) for i in range(devices) if keep(i, i ^ mask)]
        return move(value, pairs)

    other_points = move(points, [(0, 1), (1, 0)])
    first_support = move(supports, [(1, 0)])
    half = 4 * BLOCK
    padded = jnp.pad(potentials, ((0, 2 * half - columns), (0, 0)), constant_values=1.0)
    mine = jnp.where(position == 1, half, 0)
    own_pots = lax.dynamic_slice_in_dim(padded, mine, half, 0).astype(BF16)
    sent_pots = lax.dynamic_slice_in_dim(padded, half - mine, half, 0).astype(BF16)
    other_pots = move(sent_pots, [(0, 1), (1, 0)])

    payload = jnp.concatenate(
        [points[:, :LIVE], jnp.broadcast_to(supports.astype(F32), (SUP, LIVE))], axis=0
    ).astype(jnp.float16)
    far = [payload] + [swap(payload, mask) for mask in (2, 4, 6)]

    pots = pl.pallas_call(
        split_pots,
        grid=(1,),
        out_shape=[shape(BLOCK, LIVE)] * TEAM,
        in_specs=[pl.BlockSpec((columns, LIVE), lambda i: (0, 0))],
        out_specs=[pl.BlockSpec((BLOCK, LIVE), lambda i: (0, 0))] * TEAM,
        compiler_params=params(16),
        name="pots",
    )(potentials)

    def holds(source, target):
        return 2 <= source < last and target % TEAM != TEAM - 1

    pots = [pots[0]] + [swap(pots[mask], mask, holds) for mask in range(1, TEAM)]

    support_one = jnp.where(position == 1, supports, first_support).astype(F32)
    *opened, early = pl.pallas_call(
        first_step,
        out_shape=[shape(BLOCK, LIVE + LOGS)] * 4 + [shape(half, LIVE)],
        in_specs=[VMEM, VMEM, VMEM, VMEM, smem],
        out_specs=[VMEM] * 5,
        scratch_shapes=[
            scratch(dims, count, dtype=F32),
            scratch(dims, LIVE, dtype=F32),
            scratch(half, count),
            scratch(half, LIVE),
            scratch(count, depth),
            scratch(depth, LIVE),
            scratch(count, LIVE),
        ],
        compiler_params=params(24),
        name="first",
    )(points, other_points, own_pots, other_pots, support_one)
    early_other = move(early, [(0, 1)])
    arrived = [opened[0]]
    for index in range(1, 4):
        pairs = [(c, c + 2 * index) for c in range(2) if c + 2 * index < TEAM - 1]
        arrived.append(move(opened[index], pairs))

    near = [swap(value, 1) for value in far]
    slots = [None] * TEAM
    for index, mask in enumerate((0, 2, 4, 6)):
        slots[mask] = far[index].astype(F32)
        slots[mask + 1] = near[index].astype(F32)

    full = pl.BlockSpec((dims + SUP, LIVE), lambda i: (0, 0))
    kernels, seventh, team_sup, sums = pl.pallas_call(
        functools.partial(build, last),
        grid=(TEAM + 1,),
        out_shape=[
            shape(TEAM + 1, LIVE, LIVE),
            shape(dims + SUP, LIVE, dtype=F32),
            shape(TEAM, LOGS, dtype=F32),
            shape(8, LIVE, dtype=F32),
        ],
        in_specs=[full] * TEAM + [pl.BlockSpec((dims, LIVE), lambda i: (0, 1))],
        out_specs=[
            pl.BlockSpec((1, LIVE, LIVE), lambda i: (i, 0, 0)),
            full,
            pl.BlockSpec((TEAM, LOGS), lambda i: (0, 0)),
            pl.BlockSpec((8, LIVE), lambda i: (0, 0)),
        ],
        scratch_shapes=[
            scratch(TEAM, dims + SUP, LIVE, dtype=F32),
            scratch(LIVE, depth),
            scratch(depth, LIVE),
        ],
        compiler_params=params(24, True),
        name="build",
    )(*slots, points)

    def run_sweep(stage, opening, sums, incoming, previous):
        flag = (position // TEAM == stage).astype(jnp.int32).reshape(1)
        low, high = (2, TEAM - 1) if stage == 0 else (1, TEAM - 1)

        def kernel_at(i, flag):
            return (jnp.where(flag[0] == 1, jnp.clip(i, low, high), low), 0, 0)

        def whole(*dims):
            return pl.BlockSpec(dims, lambda i, flag: (0,) * len(dims))

        wide = whole(BLOCK, LIVE + LOGS)
        return pl.pallas_call(
            functools.partial(sweep, stage, teams - 1, previous is not None, len(incoming)),
            grid_spec=pltpu.PrefetchScalarGridSpec(
                num_scalar_prefetch=1,
                grid=(TEAM,),
                in_specs=[
                    pl.BlockSpec((1, LIVE, LIVE), kernel_at),
                    whole(LIVE, LIVE) if stage else whole(8, LIVE),
                    whole(TEAM, LOGS),
                    whole(8, LIVE),
                ]
                + [whole(BLOCK, LIVE)] * TEAM
                + [wide] * len(incoming)
                + [wide] * (TEAM if previous is not None else 0),
                out_specs=[wide] * (TEAM + 1),
                scratch_shapes=[
                    scratch(BLOCK, LIVE),
                    scratch(BLOCK, LOGS, dtype=F32),
                    scratch(TEAM, BLOCK, LIVE),
                    scratch(TEAM, BLOCK, LIVE),
                ],
            ),
            out_shape=[shape(BLOCK, LIVE + LOGS)] * (TEAM + 1),
            compiler_params=params(24, True),
            name="sweep%d" % min(stage, 1),
        )(flag, kernels, opening, team_sup, sums, *pots, *incoming, *(previous or []))

    before = move(
        seventh.astype(jnp.float16), [(i, i + TEAM) for i in range(devices - TEAM)]
    ).astype(F32)
    *blocks, leaving = run_sweep(0, sums, sums, arrived, None)

    for stage in range(1, teams):
        base = stage * TEAM
        incoming = move(leaving, [(base - TEAM + i, base + i) for i in range(TEAM - 1)])
        if stage == 1:
            before, sums, leaving = lax.optimization_barrier((before, sums, leaving))
            opening = pl.pallas_call(
                bridge,
                out_shape=shape(LIVE, LIVE),
                in_specs=[VMEM, VMEM],
                out_specs=VMEM,
                scratch_shapes=[scratch(LIVE, depth), scratch(depth, LIVE)],
                compiler_params=params(16),
                name="bridge",
            )(before, start_of(slots, position))
            top = devices - TEAM
            for mask in (4, 2, 1):
                sources = [i for i in range(TEAM) if i % (2 * mask) == 2 * mask - 1]
                sums = sums + move(sums, [(top + i, top + i - mask) for i in sources])
        *blocks, leaving = run_sweep(stage, opening, sums, [incoming], blocks)

    def ready(source, target):
        return source % TEAM != TEAM - 1 and target > 1

    blocks = [blocks[0]] + [swap(blocks[mask], mask, ready) for mask in range(1, TEAM)]
    lanes = pl.BlockSpec((BLOCK, LOGS), lambda i: (0, LIVE // LOGS))
    logs = pl.pallas_call(
        functools.partial(gather_logs, 1.0 / last),
        grid=(1,),
        out_shape=shape(8, TEAM * BLOCK, dtype=F32),
        in_specs=[lanes] * TEAM,
        out_specs=pl.BlockSpec((8, TEAM * BLOCK), lambda i: (0, 0)),
        scratch_shapes=[scratch(TEAM * BLOCK, LOGS, dtype=F32)],
        compiler_params=params(16),
        name="logs",
    )(*blocks)
    for team in range(teams - 1):
        shift = (teams - 1 - team) * TEAM
        moved = move(logs, [(devices - TEAM + i, devices - TEAM + i - shift) for i in range(TEAM)])
        logs = jnp.where(position // TEAM == team, moved, logs)
    log_scale = logs[0, :columns]

    messages = pl.pallas_call(
        functools.partial(finish, last),
        out_shape=shape(columns, count, dtype=F32),
        in_specs=[VMEM] * (TEAM + 2) + [smem, anywhere],
        out_specs=VMEM,
        scratch_shapes=[
            scratch(columns, LIVE),
            scratch(2, LIVE, LIVE),
            pltpu.SemaphoreType.DMA((2,)),
        ],
        compiler_params=params(24),
        name="finish",
    )(*blocks, early, early_other, supports, kernels)
    return messages[None], log_scale


def start_of(slots, position):
    device = position % TEAM
    value = slots[0]
    for mask in range(1, TEAM):
        value = jnp.where(device == mask, slots[mask], value)
    return value


def solution(mesh):
    whole = P(("groups", "tm"), None, None)
    return jax.shard_map(
        per_device,
        mesh=mesh,
        in_specs=(whole, whole, P(("groups", "tm"))),
        out_specs=(whole, P("groups")),
        check_vma=False,
    )
```

```python
import functools
import math

import jax
import jax.numpy as jnp
from jax import lax
from jax.experimental import pallas as pl
from jax.experimental.pallas import tpu as pltpu
from jax.sharding import PartitionSpec as P


A_DECAY = 0.8
EPS_SCALE = 0.05
LIVE = 1024
TEAM = 8
BLOCK = 32
LOGS = 128
SUP = 8
DEAD = -1e30

F32 = jnp.float32
BF16 = jnp.bfloat16
VMEM = pl.BlockSpec(memory_space=pltpu.VMEM)


def params(mib, grid=False):
    semantics = ("arbitrary",) if grid else None
    return pltpu.CompilerParams(vmem_limit_bytes=mib << 20, dimension_semantics=semantics)


def launch(body, **spec):
    return pl.pallas_call(body, **spec)


def block_of(device):
    return (device & 1) * 4 + (device >> 1)


def split2(value):
    high = value.astype(BF16)
    return high, (value - high.astype(F32)).astype(BF16)


def split3(value):
    high = value.astype(BF16).astype(F32)
    rest = value - high
    middle = rest.astype(BF16).astype(F32)
    return high, middle, rest - middle


def rows_of(parts):
    width = parts[0].shape[1]
    filler = jnp.zeros((16 - len(parts), width), F32)
    return jnp.concatenate([*parts, filler], axis=0).astype(BF16)


def source_features(points):
    unit = math.log2(math.e) / (2.0 * EPS_SCALE * points.shape[0])
    high, low = split2(points * (2.0 * A_DECAY * unit))
    square = jnp.sum(points * points, axis=0, keepdims=True) * (-A_DECAY * A_DECAY * unit)
    one = jnp.ones_like(square)
    return jnp.concatenate([high, high, low, rows_of((*split3(square), one, one, one))], axis=0)


def target_features(points, support, first=0):
    unit = math.log2(math.e) / (2.0 * EPS_SCALE * points.shape[0])
    high, low = split2(points)
    square = jnp.sum(points * points, axis=0, keepdims=True) * (-unit)
    one = jnp.ones_like(square)
    place = lax.broadcasted_iota(jnp.int32, square.shape, 1).astype(F32) + first
    live = place < support
    top, middle, rest = split3(square)
    top = jnp.where(live, top, DEAD)
    middle = jnp.where(live, middle, 0.0)
    rest = jnp.where(live, rest, 0.0)
    return jnp.concatenate([high, low, high, rows_of((one, one, one, top, middle, rest))], axis=0)


def fill_kernel(source, target, support, turned, features, write, first=0):
    turned[...] = source_features(source).T
    features[...] = target_features(target, support, first)
    step = 256
    for start in range(0, source.shape[1], step):
        exponent = jnp.dot(
            turned[start : start + step, :], features[...], preferred_element_type=F32
        )
        write(start, step, jnp.exp2(exponent).astype(BF16))


def log_lanes(logs):
    lane = lax.broadcasted_iota(jnp.int32, (logs.shape[0], LOGS), 1)
    high, middle, rest = split3(logs)
    third = jnp.where(lane == 2, rest, 0.0)
    return jnp.where(lane == 0, high, jnp.where(lane == 1, middle, third)).astype(BF16)


def first_step(own_ref, other_ref, pot_own, pot_other, sup_ref, *refs):
    outs, message_ref, source, target, pot_first, pot_next, turned, features, kernel = (
        refs[:4],
        *refs[4:],
    )
    position = lax.axis_index("tm")

    @pl.when(position == 0)
    def _():
        source[...] = own_ref[...]
        target[...] = other_ref[:, :LIVE]
        pot_first[...] = pot_own[...]
        pot_next[...] = pot_other[:, :LIVE]

    @pl.when(position == 1)
    def _():
        source[...] = other_ref[...]
        target[...] = own_ref[:, :LIVE]
        pot_first[...] = pot_other[...]
        pot_next[...] = pot_own[:, :LIVE]

    @pl.when(position < 2)
    def _():
        support = sup_ref[0]

        def write(start, size, values):
            kernel[start : start + size, :] = values

        fill_kernel(source[...], target[...], support, turned, features, write)
        pushed = jnp.dot(pot_first[...], kernel[...], preferred_element_type=F32)
        total = jnp.sum(pushed, axis=1, keepdims=True)
        message = pushed * (support / total)
        message_ref[...] = message.astype(BF16)
        weighted = (message * pot_next[...].astype(F32)).astype(BF16)
        logs = log_lanes(jnp.log(total / support))
        for index, out in enumerate(outs):
            rows = slice(index * BLOCK, (index + 1) * BLOCK)
            out[:, :LIVE] = weighted[rows]
            out[:, LIVE:] = logs[rows]


def split_pots(pot_ref, *outs):
    device = lax.axis_index("tm") % TEAM
    last = pot_ref.shape[0] // BLOCK - 1
    for mask, out in enumerate(outs):
        row = pl.multiple_of(jnp.minimum(block_of(device ^ mask), last) * BLOCK, BLOCK)
        out[...] = pot_ref[pl.ds(row, BLOCK), :].astype(BF16)


def build(last_position, *refs):
    slots, tail_ref = refs[:TEAM], refs[TEAM]
    kernel_ref, opening_ref, seventh_ref, sup_ref, sums_ref = refs[TEAM + 1 : TEAM + 6]
    points, turned, features = refs[TEAM + 6 :]
    position = lax.axis_index("tm")
    device, team = position % TEAM, position // TEAM
    last_team = last_position // TEAM
    dims = tail_ref.shape[0]
    step = pl.program_id(0)

    @pl.when(step == 0)
    def _():
        for mask, slot in enumerate(slots):
            points[device ^ mask] = slot[...]
        for index in range(TEAM):
            sup_ref[index : index + 1, :] = points[index, dims : dims + 1, :LOGS]
        opening_ref[...] = points[0]
        seventh_ref[...] = points[TEAM - 1]
        sums_ref[...] = jnp.zeros_like(sums_ref)

    def write(start, size, values):
        kernel_ref[0, start : start + size, :] = values

    inner = (step < TEAM - 1) & ((team > 0) | (step > 1)) & (step > 0)
    closing = (step == TEAM - 1) & ((team < last_team) | (position == last_position))

    @pl.when(inner | closing)
    def _():
        fill_kernel(
            points[step - 1, :dims, :],
            points[step, :dims, :],
            points[step, dims, 0],
            turned,
            features,
            write,
        )

    @pl.when((step == TEAM) & (position == last_position))
    def _():
        fill_kernel(
            points[TEAM - 2, :dims, :],
            tail_ref[...],
            points[TEAM - 1, dims, 0],
            turned,
            features,
            write,
            first=LIVE,
        )

    @pl.when((step >= TEAM - 1) & (position == last_position))
    def _():
        one = jnp.ones((8, LIVE), BF16)
        sums_ref[...] += lax.dot_general(
            one, kernel_ref[0], (((1,), (1,)), ((), ())), preferred_element_type=F32
        )


def bridge(before_ref, start_ref, kernel_ref, turned, features):
    @pl.when(lax.axis_index("tm") >= TEAM)
    def _():
        def write(start, size, values):
            kernel_ref[start : start + size, :] = values

        dims = before_ref.shape[0] - SUP
        fill_kernel(
            before_ref[:dims, :],
            start_ref[:dims, :],
            start_ref[dims, 0],
            turned,
            features,
            write,
        )


def sweep(stage, last_team, carried, arrivals, flag_ref, *refs):
    refs = list(refs)

    def take(count):
        taken = refs[:count]
        del refs[:count]
        return taken

    kernel_ref, opening_ref, sup_ref, sums_ref = take(4)
    pots = take(TEAM)
    incoming = take(arrivals)
    previous = take(TEAM if carried else 0)
    outs = take(TEAM)
    (leave_ref,) = take(1)
    weighted, logs, pot_all, stored = refs
    position = lax.axis_index("tm")
    device, team = position % TEAM, position // TEAM
    step = pl.program_id(0)
    first = 0 if stage else 2
    final = TEAM - 2 if stage == last_team else TEAM - 1
    active = team == stage

    @pl.when(active & (step == first))
    def _():
        for mask, pot in enumerate(pots):
            pot_all[device ^ mask] = pot[...]

        def load(ref):
            weighted[...] = ref[:, :LIVE]
            total = jnp.sum(ref[:, LIVE:].astype(F32), axis=1, keepdims=True)
            logs[...] = jnp.broadcast_to(total, logs.shape)

        if arrivals == 1:
            load(incoming[0])
        else:
            for index, ref in enumerate(incoming):
                pl.when(device >> 1 == index)(functools.partial(load, ref))

    def advance(kernel):
        support = sup_ref[pl.ds(step, 1), 0:1]
        pushed = jnp.dot(weighted[...], kernel, preferred_element_type=F32)
        total = jnp.sum(pushed, axis=1, keepdims=True)
        message = pushed * (support / total)
        stored[step] = message.astype(BF16)
        weighted[...] = (message * pot_all[step].astype(F32)).astype(BF16)
        logs[...] += jnp.log(total / support)

    if stage:
        pl.when(active & (step == 0))(lambda: advance(opening_ref[...]))
    inner = (step >= max(first, 1)) & (step <= final)
    pl.when(active & inner)(lambda: advance(kernel_ref[0]))

    @pl.when(active & (step == TEAM - 1))
    def _():
        if stage == last_team:
            support = sup_ref[TEAM - 1 : TEAM, 0:1]
            reach = jnp.sum(
                weighted[...].astype(F32) * sums_ref[0:1, :], axis=1, keepdims=True
            )
            logs[...] += jnp.log(reach / support)
            stored[TEAM - 1] = weighted[...]
        lanes = log_lanes(logs[:, 0:1])
        for mask, out in enumerate(outs):
            out[:, :LIVE] = stored[device ^ mask]
            out[:, LIVE:] = lanes
        leave_ref[:, :LIVE] = weighted[...]
        leave_ref[:, LIVE:] = lanes

    if carried:

        @pl.when((team != stage) & (step == TEAM - 1))
        def _():
            for source, out in zip(previous, outs):
                out[...] = source[...]


def gather_logs(scale, *refs):
    blocks, out_ref, column = refs[:TEAM], refs[TEAM], refs[TEAM + 1]
    device = lax.axis_index("tm") % TEAM
    for mask, block in enumerate(blocks):
        total = jnp.sum(block[...].astype(F32), axis=1, keepdims=True) * scale
        row = pl.multiple_of(block_of(device ^ mask) * BLOCK, BLOCK)
        column[pl.ds(row, BLOCK), :] = jnp.broadcast_to(total, (BLOCK, LOGS))
    out_ref[...] = column[...].T[0:8, :]


def finish(last_position, *refs):
    blocks = refs[:TEAM]
    early_own, early_other, sup_ref, kernel_ref, out_ref, weighted, halves, sem = refs[TEAM:]
    position = lax.axis_index("tm")
    device = position % TEAM
    spare = out_ref.shape[1] - LIVE
    columns = out_ref.shape[0]

    @pl.when(position == 0)
    def _():
        place = lax.broadcasted_iota(jnp.int32, out_ref.shape, 1)
        out_ref[...] = jnp.where(place < sup_ref[0], 1.0, 0.0)

    @pl.when(position == 1)
    def _():
        cut = 4 * BLOCK
        out_ref[:cut, :LIVE] = early_other[...].astype(F32)
        out_ref[cut:, :LIVE] = early_own[: columns - cut, :].astype(F32)
        out_ref[:, LIVE:] = jnp.zeros((columns, spare), F32)

    @pl.when((position > 1) & (position < last_position))
    def _():
        for mask, block in enumerate(blocks):

            @pl.when(device ^ mask < TEAM - 1)
            def _():
                row = pl.multiple_of(block_of(device ^ mask) * BLOCK, BLOCK)
                out_ref[pl.ds(row, BLOCK), :LIVE] = block[:, :LIVE].astype(F32)

        out_ref[:, LIVE:] = jnp.zeros((columns, spare), F32)

    @pl.when(position == last_position)
    def _():
        copies = []
        for half in range(2):
            copy = pltpu.make_async_copy(
                kernel_ref.at[TEAM - 1 + half], halves.at[half], sem.at[half]
            )
            copy.start()
            copies.append(copy)
        for mask in range(1, TEAM):
            row = block_of(TEAM - 1 - mask) * BLOCK
            weighted[row : row + BLOCK, :] = blocks[mask][:, :LIVE]
        total = jnp.zeros((columns, 1), F32)
        for half, copy in enumerate(copies):
            copy.wait()
            pushed = jnp.dot(weighted[...], halves[half], preferred_element_type=F32)
            out_ref[:, half * LIVE : (half + 1) * LIVE] = pushed
            total = total + jnp.sum(pushed, axis=1, keepdims=True)
        ratio = sup_ref[0].astype(F32) / total
        out_ref[...] = out_ref[...] * ratio


def shape(*dims, dtype=BF16):
    return jax.ShapeDtypeStruct(dims, dtype)


def scratch(*dims, dtype=BF16):
    return pltpu.VMEM(dims, dtype)


def per_device(points, potentials, supports):
    points, potentials = points[0], potentials[0]
    dims, count = points.shape
    columns = potentials.shape[0]
    devices = lax.axis_size("tm")
    position = lax.axis_index("tm")
    last = devices - 1
    teams = devices // TEAM
    depth = 3 * dims + 16
    smem = pl.BlockSpec(memory_space=pltpu.SMEM)
    anywhere = pl.BlockSpec(memory_space=pl.ANY)

    def move(value, pairs):
        return lax.ppermute(value, "tm", pairs)

    def swap(value, mask):
        return move(value, [(i, i ^ mask) for i in range(devices)])

    def shifted(value, steps):
        return move(value, [(i, (i + steps) % devices) for i in range(devices)])

    other_points = swap(points, 1)
    first_support = swap(supports, 1)
    half = 4 * BLOCK
    padded = jnp.pad(potentials, ((0, 2 * half - columns), (0, 0)), constant_values=1.0)
    mine = jnp.where(position == 1, half, 0)
    own_pots = lax.dynamic_slice_in_dim(padded, mine, half, 0).astype(BF16)
    sent_pots = lax.dynamic_slice_in_dim(padded, half - mine, half, 0).astype(BF16)
    other_pots = swap(sent_pots, 1)

    payload = jnp.concatenate(
        [points[:, :LIVE], jnp.broadcast_to(supports.astype(F32), (SUP, LIVE))], axis=0
    ).astype(jnp.float16)
    far = [payload] + [swap(payload, mask) for mask in (2, 4, 6)]

    pots = launch(
        split_pots,
        grid=(1,),
        out_shape=[shape(BLOCK, LIVE)] * TEAM,
        in_specs=[pl.BlockSpec((columns, LIVE), lambda i: (0, 0))],
        out_specs=[pl.BlockSpec((BLOCK, LIVE), lambda i: (0, 0))] * TEAM,
        compiler_params=params(16),
    )(potentials)

    pots = [pots[0]] + [swap(pots[mask], mask) for mask in range(1, TEAM)]

    support_one = jnp.where(position == 1, supports, first_support).astype(F32)
    *opened, early = launch(
        first_step,
        out_shape=[shape(BLOCK, LIVE + LOGS)] * 4 + [shape(half, LIVE)],
        in_specs=[VMEM, VMEM, VMEM, VMEM, smem],
        out_specs=[VMEM] * 5,
        scratch_shapes=[
            scratch(dims, count, dtype=F32),
            scratch(dims, LIVE, dtype=F32),
            scratch(half, count),
            scratch(half, LIVE),
            scratch(count, depth),
            scratch(depth, LIVE),
            scratch(count, LIVE),
        ],
        compiler_params=params(24),
    )(points, other_points, own_pots, other_pots, support_one)
    early_other = swap(early, 1)
    arrived = [opened[0]]
    for index in range(1, 4):
        arrived.append(swap(opened[index], 2 * index))

    near = [swap(value, 1) for value in far]
    slots = [None] * TEAM
    for index, mask in enumerate((0, 2, 4, 6)):
        slots[mask] = far[index].astype(F32)
        slots[mask + 1] = near[index].astype(F32)

    full = pl.BlockSpec((dims + SUP, LIVE), lambda i: (0, 0))
    kernels, opening, seventh, team_sup, sums = launch(
        functools.partial(build, last),
        grid=(TEAM + 1,),
        out_shape=[
            pltpu.HBM((TEAM + 1, LIVE, LIVE), BF16),
            shape(dims + SUP, LIVE, dtype=F32),
            shape(dims + SUP, LIVE, dtype=F32),
            shape(TEAM, LOGS, dtype=F32),
            shape(8, LIVE, dtype=F32),
        ],
        in_specs=[full] * TEAM + [pl.BlockSpec((dims, LIVE), lambda i: (0, 1))],
        out_specs=[
            pl.BlockSpec((1, LIVE, LIVE), lambda i: (i, 0, 0)),
            full,
            full,
            pl.BlockSpec((TEAM, LOGS), lambda i: (0, 0)),
            pl.BlockSpec((8, LIVE), lambda i: (0, 0)),
        ],
        scratch_shapes=[
            scratch(TEAM, dims + SUP, LIVE, dtype=F32),
            scratch(LIVE, depth),
            scratch(depth, LIVE),
        ],
        compiler_params=params(24, True),
    )(*slots, points)

    kernels = pltpu.with_memory_space_constraint(kernels, pltpu.HBM)

    def run_sweep(stage, opening, sums, incoming, previous):
        flag = (position // TEAM == stage).astype(jnp.int32).reshape(1)
        low, high = (2, TEAM - 1) if stage == 0 else (1, TEAM - 1)

        def kernel_at(i, flag):
            return (jnp.where(flag[0] == 1, jnp.clip(i, low, high), low), 0, 0)

        def whole(*dims):
            return pl.BlockSpec(dims, lambda i, flag: (0,) * len(dims))

        wide = whole(BLOCK, LIVE + LOGS)
        return launch(
            functools.partial(sweep, stage, teams - 1, previous is not None, len(incoming)),
            grid_spec=pltpu.PrefetchScalarGridSpec(
                num_scalar_prefetch=1,
                grid=(TEAM,),
                in_specs=[
                    pl.BlockSpec((1, LIVE, LIVE), kernel_at),
                    whole(LIVE, LIVE) if stage else whole(8, LIVE),
                    whole(TEAM, LOGS),
                    whole(8, LIVE),
                ]
                + [whole(BLOCK, LIVE)] * TEAM
                + [wide] * len(incoming)
                + [wide] * (TEAM if previous is not None else 0),
                out_specs=[wide] * (TEAM + 1),
                scratch_shapes=[
                    scratch(BLOCK, LIVE),
                    scratch(BLOCK, LOGS, dtype=F32),
                    scratch(TEAM, BLOCK, LIVE),
                    scratch(TEAM, BLOCK, LIVE),
                ],
            ),
            out_shape=[shape(BLOCK, LIVE + LOGS)] * (TEAM + 1),
            compiler_params=params(24, True),
        )(flag, kernels, opening, team_sup, sums, *pots, *incoming, *(previous or []))

    before = shifted(seventh.astype(jnp.float16), TEAM).astype(F32)
    *blocks, leaving = run_sweep(0, sums, sums, arrived, None)

    for stage in range(1, teams):
        base = stage * TEAM
        incoming = move(leaving, [(base - TEAM + i, base + i) for i in range(TEAM - 1)])
        if stage == 1:
            before, sums, leaving = lax.optimization_barrier((before, sums, leaving))
            opening = launch(
                bridge,
                out_shape=shape(LIVE, LIVE),
                in_specs=[VMEM, VMEM],
                out_specs=VMEM,
                scratch_shapes=[scratch(LIVE, depth), scratch(depth, LIVE)],
                compiler_params=params(16),
            )(before, opening)
            for mask in (4, 2, 1):
                sums = sums + swap(sums, mask)
        *blocks, leaving = run_sweep(stage, opening, sums, [incoming], blocks)

    blocks = [blocks[0]] + [swap(blocks[mask], mask) for mask in range(1, TEAM)]
    lanes = pl.BlockSpec((BLOCK, LOGS), lambda i: (0, LIVE // LOGS))
    logs = launch(
        functools.partial(gather_logs, 1.0 / last),
        grid=(1,),
        out_shape=shape(8, TEAM * BLOCK, dtype=F32),
        in_specs=[lanes] * TEAM,
        out_specs=pl.BlockSpec((8, TEAM * BLOCK), lambda i: (0, 0)),
        scratch_shapes=[scratch(TEAM * BLOCK, LOGS, dtype=F32)],
        compiler_params=params(16),
    )(*blocks)
    for team in range(teams - 1):
        shift = (teams - 1 - team) * TEAM
        moved = shifted(logs, -shift)
        logs = jnp.where(position // TEAM == team, moved, logs)
    log_scale = logs[0, :columns]

    messages = launch(
        functools.partial(finish, last),
        out_shape=shape(columns, count, dtype=F32),
        in_specs=[VMEM] * (TEAM + 2) + [smem, anywhere],
        out_specs=VMEM,
        scratch_shapes=[
            scratch(columns, LIVE),
            scratch(2, LIVE, LIVE),
            pltpu.SemaphoreType.DMA((2,)),
        ],
        compiler_params=params(24),
    )(*blocks, early, early_other, supports, kernels)
    return messages[None], log_scale


def solution(mesh):
    whole = P(("groups", "tm"), None, None)
    return jax.shard_map(
        per_device,
        mesh=mesh,
        in_specs=(whole, whole, P(("groups", "tm"))),
        out_specs=(whole, P("groups")),
        check_vma=False,
    )
```
